512 devices in a mesh: expert: 32 (over z, core), replica: 16 (over x, y).
Axes of the slice: x: 4, y: 4, z: 16, core: 2. Of those that a mesh axis runs over, the one named last changes fastest.
Arguments:
- weights: bfloat16 [32, 3, 2048, 512], P('expert', None, 'replica'), may hold values from -0.125 to 0.125
- first_moment: float32 [32, 3, 2048, 512], P('expert', None, 'replica'), may hold values from -128 to 128
- second_moment: float32 [32, 3, 2048, 512], P('expert', None, 'replica'), may hold values from 100 to 100000
- out_grads: bfloat16 [16, 4096, 2048], P('replica', 'expert'), may hold values from -8 to 8
- routes: int32 [16, 4096, 1], P('replica', 'expert'), may hold values from 0 to 31; in each aligned block of 128 rows (0 to 127, 128 to 255, ..., all dimensions but the last counted through in order) at most 8 rows name the same one
- task_ids: int32 [16, 32], P('replica', 'expert'), may hold values from 0 to 7
- task_weights: float32 [8], replicated, may hold values from 0.25 to 4
- saved_inputs: bfloat16 [16, 32, 256, 2048], P('replica', 'expert'), may hold values from -8 to 8
Outputs:
- input_grads: bfloat16 [16, 4096, 2048], P('replica', 'expert')
- adam_step: float32 [32, 3, 2048, 512], P('expert', None, 'replica')
The draws below stay inside these ranges and needn't reach their ends.
Inputs may be any that keep to these rules, and one draw needn't show every extreme that they name: `routes`: at most 8 of the rows of one device go to one expert, and in every draw some device sends exactly 8 rows to some expert.
All inputs are finite; a program needn't handle non-finite values.
Results may differ from the reference program's by a relative error of at most 0.0057.
Values may be sent and summed in bfloat16 or wider, within the bound.
A program may use at most 128 MiB of HBM per device.

```python
import math
import jax
import jax.numpy as jnp
import numpy as np
from jax import lax

D = 2048
F = 512
TOK_DEV = 128
BLOCK = 128
TASKS = 8
EXPERTS = 32
REPLICAS = 16
CAP = 8
SLOTS = 256
TOKENS = 4096
BLOCKS = 32


def segment_strength(key):
    levels = REPLICAS.bit_length() - 1
    flip_mask = jax.random.randint(jax.random.fold_in(key, 31), (), 0, REPLICAS, dtype=jnp.int32)
    labels = jnp.bitwise_xor(jnp.arange(REPLICAS, dtype=jnp.int32), flip_mask)
    seg_order = jnp.zeros((REPLICAS,), jnp.int32)
    for bit_pos in range(levels):
        seg_order = seg_order + (labels >> bit_pos & 1) * 2 ** (levels - 1 - bit_pos)
    fraction = seg_order.astype(jnp.float32) / float(max(REPLICAS - 1, 1))
    jitter = jax.random.uniform(jax.random.fold_in(key, 33), (REPLICAS,), jnp.float32, -0.3, 0.3)
    seg_level = jnp.exp(math.log(0.06) + fraction * math.log(2.0 / 0.06) + jitter)
    column_segment = jnp.arange(D, dtype=jnp.int32) // (D // REPLICAS)
    return seg_level[column_segment]


def common_part(key, length, salt):
    base_part = jax.random.normal(jax.random.fold_in(key, salt), (length,), jnp.float32)
    spread = jnp.exp(jax.random.uniform(jax.random.fold_in(key, salt + 1), (length,), jnp.float32, 0.0, math.log(2.5)))
    return base_part * spread * segment_strength(key)


def draw_out_grads(key, part):
    shared = common_part(key, D, 11)
    noise_part = jax.random.normal(jax.random.fold_in(key, 13), (REPLICAS, TOKENS, D), jnp.float32)
    return jnp.clip(noise_part + shared[None, None, :], -8.0, 8.0).astype(jnp.bfloat16)


def draw_saved_inputs(key, part):
    shared = common_part(key, D, 21)
    row_scale = jnp.exp(jax.random.uniform(jax.random.fold_in(key, 23), (REPLICAS, EXPERTS, SLOTS, 1), jnp.float32, 0.0, math.log(4.0)))
    noise_part = jax.random.normal(jax.random.fold_in(key, 25), (REPLICAS, EXPERTS, SLOTS, D), jnp.float32)
    return jnp.clip(noise_part * row_scale + shared[None, None, None, :], -8.0, 8.0).astype(jnp.bfloat16)


def with_ends(values, rng, low, high):
    place = [jax.random.randint(jax.random.fold_in(rng, axis), (), 0, length) for axis, length in enumerate(values.shape)]
    longest = values.shape.index(max(values.shape))
    next_to = place[:longest] + [(place[longest] + 1) % values.shape[longest]] + place[longest + 1:]
    return values.at[tuple(place)].set(low).at[tuple(next_to)].set(high)


def steps_of(stream_key, dims, cuts, smallest, largest):
    def one(position, parts):
        draws = jax.random.uniform(jax.random.fold_in(jax.random.fold_in(stream_key, 6), position), (parts,), jnp.float32, smallest / len(cuts), largest / len(cuts))
        return jnp.repeat(jnp.exp(draws), dims[position] // parts).reshape((-1,) + (1,) * (len(dims) - position - 1))

    gain = one(*cuts[0])
    for cut in cuts[1:]:
        gain = gain * one(*cut)
    return gain


def deal_out(stream_key, own, number, rows, amount, top, reach, lean):
    ranking = jax.random.permutation(stream_key, amount)
    packed, usual = load_shares(amount, rows * top, reach, lean, True), load_shares(amount, rows * top, reach, lean, False)
    places = jnp.arange(amount)

    def named(sizes, rotation):
        used = int((sizes > 0).sum())
        fixed = max(1, used // 4)
        shifted = fixed + (places - fixed + rotation * (used - fixed)) % max(1, amount - fixed)
        return jnp.zeros((amount,), jnp.int32).at[ranking[jnp.where(places < fixed, places, shifted)]].set(jnp.asarray(sizes, jnp.int32))

    sizes = jnp.where(number % 4 == 0, named(packed, number // 4), named(usual, number - number // 4 - 1))
    mixed = jax.random.permutation(jax.random.fold_in(own, 3), amount)
    source_of, sink = mixed[0:amount // 2 * 2:2], mixed[1:amount // 2 * 2:2]
    margin = jnp.minimum(sizes[source_of] - 1, reach - sizes[sink]) // 2
    margin = jnp.where((source_of == ranking[0]) | (sink == ranking[0]) | (sizes[sink] == 0), 0, jnp.maximum(margin, 0))
    shifted = jax.random.randint(jax.random.fold_in(own, 4), (amount // 2,), 0, 1 << 20) % (margin + 1)
    sizes = sizes.at[source_of].add(-shifted).at[sink].add(shifted)
    items = jnp.searchsorted(jnp.cumsum(sizes), jnp.arange(rows * top), side="right").astype(jnp.int32)
    table = items.reshape(top, rows).T
    table = table[jax.random.permutation(jax.random.fold_in(own, 1), rows)]
    rotation = jax.random.randint(jax.random.fold_in(own, 2), (rows, 1), 0, top)
    return jnp.take_along_axis(table, (jnp.arange(top)[None, :] + rotation) % top, axis=1)


def load_shares(count, total, bound, slope, full):
    portions = [(1 << 20) // math.isqrt(grade ** slope) + 1 for grade in range(1, count + 1)]
    largest = bound if full else min(bound, max(-(-total // count), total * portions[0] // sum(portions)))
    least = 1 if total - largest >= count - 1 else 0
    holding, surplus = [largest] + [least] * (count - 1), total - largest - least * (count - 1)
    while surplus > 0:
        movable = [i for i in range(1, count) if holding[i] < largest] or [i for i in range(1, count) if holding[i] < bound]
        whole, budget = sum([portions[i] for i in movable]), surplus
        for i in movable:
            extra = min(bound - holding[i], max(1, budget * portions[i] // whole), surplus)
            holding[i] = holding[i] + extra
            surplus = surplus - extra
    return np.array(holding)


def scatter_about(rng, extent, width, reach, pieces=(), held_as=jnp.bfloat16):
    drawn = width * jax.random.normal(rng, extent, jnp.float32)
    if pieces:
        drawn = drawn * steps_of(rng, extent, pieces, -0.22, 0.18)
    return jnp.clip(drawn, -reach, reach).astype(held_as)


def setup_inputs(seed: int = 0) -> dict:
    key_list = jax.random.split(jax.random.key(seed), 9)
    weights = scatter_about(key_list[0], (EXPERTS, 3, D, F), D ** -0.5, 0.125, ((0, 32), (2, 16)))
    first_moment = scatter_about(key_list[1], (EXPERTS, 3, D, F), 20.0, 128.0, ((0, 32), (2, 16)), jnp.float32)
    second_moment = jnp.clip(jnp.exp(math.log(100000.0) - 6.9077553 * jax.random.uniform(key_list[2], (EXPERTS, 3, D, F), jnp.float32) ** steps_of(key_list[2], (EXPERTS, 3, D, F), ((0, 32), (2, 16)), -0.2, 0.2)), 100.0, 100000.0)
    out_grads = draw_out_grads(jax.random.fold_in(key_list[8], 71), 0)
    routes_keys = jax.random.split(jax.random.fold_in(key_list[4], 1), REPLICAS * TOKENS // TOK_DEV)
    routes_turns = jax.random.permutation(jax.random.fold_in(key_list[4], 3), REPLICAS * TOKENS // TOK_DEV)
    routes = jax.vmap(lambda own, number: deal_out(jax.random.fold_in(key_list[4], 2), own, number, TOK_DEV, EXPERTS, 1, CAP, 2))(routes_keys, routes_turns).reshape((REPLICAS, TOKENS, 1))
    task_ids = with_ends(jax.random.randint(key_list[5], (REPLICAS, BLOCKS), 0, TASKS), jax.random.fold_in(key_list[5], 1), 0, TASKS - 1).astype(jnp.int32)
    task_weights = jnp.clip(jnp.exp(jax.random.uniform(key_list[6], (TASKS,), jnp.float32, math.log(0.25), math.log(4.0))), 0.25, 4.0)
    saved_inputs = draw_saved_inputs(jax.random.fold_in(key_list[8], 71), 0)
    return {"weights": weights, "first_moment": first_moment, "second_moment": second_moment, "out_grads": out_grads, "routes": routes, "task_ids": task_ids, "task_weights": task_weights, "saved_inputs": saved_inputs}


beta_first = 0.9
beta_second = 0.95
adam_eps = 1e-08
norm_eps = 1e-06
first_fix = 1.0 - (0.9 ** 50) ** 2
second_fix = 1.0 - (0.95 ** 50) ** 2

def round_half(values):
    narrow = values.astype(jnp.bfloat16)
    narrow = lax.optimization_barrier(narrow)
    return narrow.astype(jnp.float32)

def slot_layout(routes):
    expert_of = routes[:, :, 0].reshape(REPLICAS, EXPERTS, TOK_DEV).astype(jnp.int32)
    chosen = (expert_of[..., None] == jnp.arange(EXPERTS, dtype=jnp.int32)).astype(jnp.int32)
    before = (jnp.cumsum(chosen, axis=2) - chosen).astype(jnp.int32)
    slot_rank = lax.optimization_barrier(jnp.sum(before * chosen, axis=3)).astype(jnp.int32)
    source = jnp.arange(EXPERTS, dtype=jnp.int32)[None, :, None]
    slot_index = (source * CAP + slot_rank).astype(jnp.int32)
    return (expert_of.reshape(REPLICAS, TOKENS), slot_index.reshape(REPLICAS, TOKENS))

def adasum(grads):
    segment = jnp.arange(D, dtype=jnp.int32) // (D // REPLICAS)
    current = grads
    levels = REPLICAS.bit_length() - 1
    for level_now in range(levels):
        paired = current.reshape(current.shape[0] // 2, 2, 3, D, F)
        first_side = paired[:, 0]
        second_side = paired[:, 1]
        low_half = (segment >> level_now & 1 == 0)[None, None, :, None]
        side_first = jnp.where(low_half, first_side, round_half(first_side))
        side_second = jnp.where(low_half, round_half(second_side), second_side)
        cross_sum = lax.optimization_barrier(jnp.sum(side_first * side_second, axis=(1, 2, 3)))
        norm_first = lax.optimization_barrier(jnp.sum(side_first * side_first, axis=(1, 2, 3)))
        norm_second = lax.optimization_barrier(jnp.sum(side_second * side_second, axis=(1, 2, 3)))
        coef_first = 1.0 - cross_sum / (2.0 * (norm_first + norm_eps))
        coef_second = 1.0 - cross_sum / (2.0 * (norm_second + norm_eps))
        current = coef_first[:, None, None, None] * side_first + coef_second[:, None, None, None] * side_second
    return current[0]

def expert_step(operands):
    weight_e, inputs_e, incoming_e, moment_one, moment_two = operands
    weight_wide = weight_e.astype(jnp.float32)
    inputs_wide = inputs_e.astype(jnp.float32)
    incoming_wide = incoming_e.astype(jnp.float32)
    gate_pre = jnp.einsum('rsd,df->rsf', inputs_wide, weight_wide[0])
    up_pre = jnp.einsum('rsd,df->rsf', inputs_wide, weight_wide[1])
    gate_act = jax.nn.silu(gate_pre)
    hidden = (gate_act * up_pre).astype(jnp.bfloat16)
    hidden_grad = jnp.einsum('rsd,df->rsf', incoming_wide, weight_wide[2])
    sigmoid_gate = jax.nn.sigmoid(gate_pre)
    gate_grad = (hidden_grad * up_pre * sigmoid_gate * (1.0 + gate_pre * (1.0 - sigmoid_gate))).astype(jnp.bfloat16)
    up_grad = (hidden_grad * gate_act).astype(jnp.bfloat16)
    gate_wide = gate_grad.astype(jnp.float32)
    up_wide = up_grad.astype(jnp.float32)
    slot_grads = (jnp.einsum('rsf,df->rsd', gate_wide, weight_wide[0]) + jnp.einsum('rsf,df->rsd', up_wide, weight_wide[1])).astype(jnp.bfloat16)
    grads = jnp.stack([jnp.einsum('rsd,rsf->rdf', inputs_wide, gate_wide), jnp.einsum('rsd,rsf->rdf', inputs_wide, up_wide), jnp.einsum('rsd,rsf->rdf', incoming_wide, hidden.astype(jnp.float32))], axis=1)
    merged = adasum(grads)
    first_new = beta_first * moment_one + (1.0 - beta_first) * merged
    second_new = beta_second * moment_two + (1.0 - beta_second) * merged * merged
    adam_step = first_new / first_fix / (jnp.sqrt(second_new / second_fix) + adam_eps)
    return (slot_grads, adam_step)

def reference(weights, first_moment, second_moment, out_grads, routes, task_ids, task_weights, saved_inputs):
    expert_of, slot_index = slot_layout(routes)
    block_weight = task_weights[task_ids]
    scaled = (out_grads.astype(jnp.float32).reshape(REPLICAS, BLOCKS, BLOCK, D) * block_weight[:, :, None, None]).reshape(REPLICAS, TOKENS, D).astype(jnp.bfloat16)
    replica_of = jnp.broadcast_to(jnp.arange(REPLICAS, dtype=jnp.int32)[:, None], (REPLICAS, TOKENS))
    received = jnp.zeros((EXPERTS, REPLICAS, SLOTS, D), jnp.bfloat16).at[expert_of, replica_of, slot_index].set(scaled)
    inputs_by_expert = jnp.swapaxes(saved_inputs, 0, 1)
    slot_grads, adam_step = lax.map(expert_step, (weights, inputs_by_expert, received, first_moment, second_moment))
    input_grads = slot_grads[expert_of, replica_of, slot_index]
    return (input_grads, adam_step)
```

```python
import functools

import jax
import jax.numpy as jnp
from jax import lax
from jax.experimental import pallas as pl
from jax.experimental.pallas import tpu as pltpu
from jax.sharding import PartitionSpec as P

beta_first = 0.9
beta_second = 0.95
adam_eps = 1e-08
norm_eps = 1e-06
first_fix = 1.0 - (0.9**50) ** 2
second_fix = 1.0 - (0.95**50) ** 2

F32 = jnp.float32
BF16 = jnp.bfloat16


def dot_rows(left, right):
    return lax.dot_general(left, right, (((0,), (0,)), ((), ())), preferred_element_type=F32)


def dot_last(left, right):
    return lax.dot_general(left, right, (((1,), (1,)), ((), ())), preferred_element_type=F32)


def iota(shape, axis):
    return lax.broadcasted_iota(jnp.int32, shape, axis)


def kernel(
    experts, nx, ny,
    w_ref, fm_ref, sm_ref, og_ref, route_ref, tid_ref, tw_ref, x_ref,
    ig_ref, step_ref,
    place, out3, in3, ret3, back3, rows, wfull, gact, upfac, gg, ug, hid, vsend, vbuf, acc, gsend, gbuf,
    a_send, a_recv, b_send, b_recv, w_send, w_recv, v_send, v_recv, g_send, g_recv,
):
    reps = nx * ny
    me_e = lax.axis_index("expert")
    me_r = lax.axis_index("replica")
    mx, my = me_r // ny, me_r % ny
    row_count, width = og_ref.shape
    slots = x_ref.shape[0]
    cap = slots // experts
    hidden = w_ref.shape[2]
    seg = w_ref.shape[1]
    half = seg // 2

    barrier = pltpu.get_barrier_semaphore()

    @pl.loop(1, experts)
    def _(i):
        pl.semaphore_signal(barrier, inc=1, device_id={"expert": (me_e + i) % experts, "replica": me_r})

    @pl.loop(1, reps)
    def _(i):
        pl.semaphore_signal(barrier, inc=1, device_id={"expert": me_e, "replica": (me_r + i) % reps})

    scale = tw_ref[tid_ref[0, 0]]
    expert_of = route_ref[...]
    chosen = (iota((experts, row_count), 0) == expert_of).astype(F32)
    earlier = (iota((row_count, row_count), 0) < iota((row_count, row_count), 1)).astype(BF16)
    before = jnp.dot(chosen.astype(BF16), earlier, preferred_element_type=F32)
    rank = jnp.sum(before * chosen, axis=0, keepdims=True)
    slot = expert_of * cap + rank.astype(jnp.int32)
    place[...] = (iota((slots, row_count), 0) == slot).astype(BF16)
    cols = min(512, width)
    for c in range(0, width, cols):
        scaled = (og_ref[:, c : c + cols].astype(F32) * scale).astype(BF16)
        moved = jnp.dot(place[...], scaled, preferred_element_type=F32)
        out3[:, :, c : c + cols] = moved.reshape(experts, cap, cols).astype(BF16)

    wfull[:, mx, my] = w_ref[...]
    pl.semaphore_wait(barrier, experts - 1 + reps - 1)

    def stage_one(k, along_y):
        lo = 0 if along_y else half
        idx = (0 if along_y else ny - 1) + k - 1
        to = mx * ny + (my + k) % ny if along_y else ((mx + k) % nx) * ny + my
        part = wfull.at[:, mx, my, lo : lo + half]
        return pltpu.make_async_remote_copy(
            src_ref=w_ref.at[:, lo : lo + half], dst_ref=part, send_sem=w_send.at[idx], recv_sem=w_recv.at[idx],
            device_id={"expert": me_e, "replica": to},
        )

    def stage_two(k, along_y, group):
        lo = half if along_y else 0
        base = (ny - 1) + (nx - 1)
        idx = base + (0 if along_y else ny - 1) + k - 1 + group * base
        to = mx * ny + (my + k) % ny if along_y else ((mx + k) % nx) * ny + my
        mats = pl.ds(0, 2) if group == 0 else pl.ds(2, 1)
        if along_y:
            part = wfull.at[mats, :, my, lo : lo + half]
        else:
            part = wfull.at[mats, mx, :, lo : lo + half]
        return pltpu.make_async_remote_copy(
            src_ref=part, dst_ref=part, send_sem=w_send.at[idx], recv_sem=w_recv.at[idx],
            device_id={"expert": me_e, "replica": to},
        )

    ones = [stage_one(k, True) for k in range(1, ny)] + [stage_one(k, False) for k in range(1, nx)]
    for c in ones:
        c.start()

    def row_copy(i, src, dst, send, recv):
        to = (me_e + i) % experts
        return pltpu.make_async_remote_copy(
            src_ref=src.at[to], dst_ref=dst.at[me_e], send_sem=send.at[i], recv_sem=recv.at[i],
            device_id={"expert": to, "replica": me_r},
        )

    def row_order(n):
        return (n + experts // 2) % experts

    @pl.loop(0, experts)
    def _(n):
        i = row_order(n)

        @pl.when(i != 0)
        def _():
            row_copy(i, out3, in3, a_send, a_recv).start()

    in3[me_e] = out3[me_e]

    for c in ones:
        c.wait_recv()
    twos = [
        [stage_two(k, True, g) for k in range(1, ny)] + [stage_two(k, False, g) for k in range(1, nx)]
        for g in range(2)
    ]
    for g in range(2):
        for c in twos[g]:
            c.start()

    for c in twos[0]:
        c.wait_recv()

    def weight(i):
        return wfull[i].reshape(reps * seg, hidden)

    xs = x_ref[...]
    gact[...] = jnp.dot(xs, weight(0), preferred_element_type=F32)
    upfac[...] = jnp.dot(xs, weight(1), preferred_element_type=F32)
    step_rows = 16

    @pl.loop(0, slots // step_rows)
    def _(n):
        at = pl.ds(pl.multiple_of(n * step_rows, step_rows), step_rows)
        gate, up = gact[at], upfac[at]
        sig = jax.nn.sigmoid(gate)
        act = gate * sig
        hid[at] = (act * up).astype(BF16)
        upfac[at] = up * sig * (1.0 + gate * (1.0 - sig))
        gact[at] = act

    for c in twos[1]:
        c.wait_recv()

    @pl.loop(1, experts)
    def _(i):
        row_copy(i, out3, in3, a_send, a_recv).wait_recv()

    def flat_rows(src):
        @pl.loop(0, slots // 16)
        def _(n):
            per = 16 // cap
            got = src[pl.ds(n * per, per)].astype(F32).reshape(16, width)
            rows[pl.ds(pl.multiple_of(n * 16, 16), 16)] = got.astype(BF16)

    flat_rows(in3)
    gact_now = jnp.dot(rows[...], weight(2), preferred_element_type=F32)
    gg[...] = (gact_now * upfac[...]).astype(BF16)
    ug[...] = (gact_now * gact[...]).astype(BF16)

    def offsets(k):
        i, j = k // ny, k % ny
        return (nx // 2 + (nx - 1) * i) % nx, (ny // 2 + (ny - 1) * j) % ny

    own_k = (nx // 2) * ny + ny // 2

    def seg_copy(k):
        dx, dy = offsets(k)
        to = ((mx + dx) % nx) * ny + (my + dy) % ny
        return pltpu.make_async_remote_copy(
            src_ref=vsend.at[to], dst_ref=vbuf.at[me_r], send_sem=v_send.at[k], recv_sem=v_recv.at[k],
            device_id={"expert": me_e, "replica": to},
        )

    def make_segment(k):
        dx, dy = offsets(k)
        to = ((mx + dx) % nx) * ny + (my + dy) % ny
        at = pl.ds(pl.multiple_of(to * seg, seg), seg)
        x_part = x_ref[:, at]
        vsend[to, 0:seg] = dot_rows(x_part, gg[...]).astype(BF16)
        vsend[to, seg : 2 * seg] = dot_rows(x_part, ug[...]).astype(BF16)
        vsend[to, 2 * seg : 3 * seg] = dot_rows(rows[:, at], hid[...]).astype(BF16)

        @pl.when(k != own_k)
        def _():
            seg_copy(k).start()

        @pl.when(k == own_k)
        def _():
            vbuf[me_r] = vsend[me_r]

    first_part = max(1, reps // 4)
    pl.loop(0, first_part)(make_segment)

    per = min(2, reps)

    @pl.loop(0, reps // per)
    def _(n):
        g_part = wfull[0, n * per // ny, pl.ds((n * per) % ny, per)].reshape(per * seg, hidden)
        u_part = wfull[1, n * per // ny, pl.ds((n * per) % ny, per)].reshape(per * seg, hidden)
        total = dot_last(gg[...], g_part) + dot_last(ug[...], u_part)
        at = pl.ds(pl.multiple_of(n * per * seg, per * seg), per * seg)
        ret3[:, :, at] = total.reshape(experts, cap, per * seg).astype(BF16)

    @pl.loop(1, experts)
    def _(i):
        row_copy(i, out3, in3, a_send, a_recv).wait_send()

    @pl.loop(0, experts)
    def _(n):
        i = row_order(n)

        @pl.when(i != 0)
        def _():
            row_copy(i, ret3, back3, b_send, b_recv).start()

    back3[me_e] = ret3[me_e]

    pl.loop(first_part, reps)(make_segment)

    def from_replica(k):
        dx, dy = offsets(k)
        return ((mx + nx - dx) % nx) * ny + (my + ny - dy) % ny

    block = 32
    lanes = hidden // 128

    @pl.loop(0, reps)
    def _(k):
        @pl.when(k != own_k)
        def _():
            seg_copy(k).wait_recv()

        r = from_replica(k)

        @pl.loop(0, k + 1)
        def _(j):
            s = from_replica(j)

            def add_block(n, total):
                at = pl.ds(pl.multiple_of(n * block, block), block)
                product = vbuf[r, at].astype(F32) * vbuf[s, at].astype(F32)
                for c in range(lanes):
                    column = product[:, c * 128 : (c + 1) * 128]
                    total = total + jnp.sum(column.reshape(block // 8, 8, 128), axis=0)
                return total

            total = lax.fori_loop(0, 3 * seg // block, add_block, jnp.zeros((8, 128), F32))
            acc[r * reps + s] = total
            acc[s * reps + r] = total

    lane = iota((reps, 128), 1)
    gram = jnp.zeros((reps, 128), F32)
    for r in range(reps):
        part = jnp.sum(acc[r * reps : (r + 1) * reps], axis=1)
        gram = gram + jnp.where(lane == r, jnp.sum(part, axis=1, keepdims=True), 0.0)
    gsend[...] = gram
    gbuf[me_r] = gram

    def gram_copy(i):
        to = (me_r + i) % reps
        return pltpu.make_async_remote_copy(
            src_ref=gsend, dst_ref=gbuf.at[me_r], send_sem=g_send.at[i], recv_sem=g_recv.at[i],
            device_id={"expert": me_e, "replica": to},
        )

    pl.loop(1, reps)(lambda i: gram_copy(i).start())

    @pl.loop(1, experts)
    def _(i):
        row_copy(i, ret3, back3, b_send, b_recv).wait_recv()

    flat_rows(back3)
    for c in range(0, width, cols):
        ig_ref[:, c : c + cols] = dot_rows(place[...], rows[:, c : c + cols]).astype(BF16)

    pl.loop(1, reps)(lambda i: gram_copy(i).wait_recv())
    total = gbuf[0]
    for r in range(1, reps):
        total = total + gbuf[r]
    gram = total[:, 0:reps]
    low, high = iota((reps, reps), 0), iota((reps, reps), 1)
    c_col = jnp.ones((reps, 1), F32)
    c_row = jnp.ones((1, reps), F32)
    for level in range(reps.bit_length() - 1):
        now = c_col * c_row * gram
        same = (low >> level) == (high >> level)
        pair = ((low >> (level + 1)) == (high >> (level + 1))) & jnp.logical_not(same)
        own = jnp.where(same, now, 0.0)
        other = jnp.where(pair, now, 0.0)
        own_row, own_col = jnp.sum(own, axis=0, keepdims=True), jnp.sum(own, axis=1, keepdims=True)
        ab_row, ab_col = jnp.sum(other, axis=0, keepdims=True), jnp.sum(other, axis=1, keepdims=True)
        norm_col = jnp.sum(jnp.where(same, own_row, 0.0), axis=1, keepdims=True)
        norm_row = jnp.sum(jnp.where(same, own_col, 0.0), axis=0, keepdims=True)
        cross_col = jnp.sum(jnp.where(same, ab_row, 0.0), axis=1, keepdims=True)
        cross_row = jnp.sum(jnp.where(same, ab_col, 0.0), axis=0, keepdims=True)
        c_col = c_col * (1.0 - cross_col / (2.0 * (norm_col + norm_eps)))
        c_row = c_row * (1.0 - cross_row / (2.0 * (norm_row + norm_eps)))

    coefs = [c_row[:, r : r + 1] for r in range(reps)]

    for m in range(3):

        @pl.loop(0, seg // 16)
        def _(n):
            src = pl.ds(pl.multiple_of(m * seg + n * 16, 16), 16)
            at = pl.ds(pl.multiple_of(n * 16, 16), 16)
            merged = jnp.zeros((16, hidden), F32)
            for r in range(reps):
                merged = merged + coefs[r] * vbuf[r, src].astype(F32)
            first = beta_first * fm_ref[m, at] + (1.0 - beta_first) * merged
            second = beta_second * sm_ref[m, at] + (1.0 - beta_second) * merged * merged
            step_ref[m, at] = first / first_fix / (jnp.sqrt(second / second_fix) + adam_eps)

    for c in ones + twos[0] + twos[1]:
        c.wait_send()

    @pl.loop(1, experts)
    def _(i):
        row_copy(i, ret3, back3, b_send, b_recv).wait_send()

    @pl.loop(0, reps)
    def _(k):
        @pl.when(k != own_k)
        def _():
            seg_copy(k).wait_send()

    pl.loop(1, reps)(lambda i: gram_copy(i).wait_send())


def grid_of(reps):
    ny = 1 << ((reps.bit_length() - 1) // 2)
    return reps // ny, ny


def shards(
    weights, first_moment, second_moment, out_grads, routes, task_ids, task_weights, saved_inputs
):
    experts = lax.axis_size("expert")
    reps = lax.axis_size("replica")
    nx, ny = grid_of(reps)
    row_count, width = out_grads.shape[1:]
    _, mats, seg, hidden = weights.shape
    slots = saved_inputs.shape[2]
    cap = slots // experts
    vmem = pl.BlockSpec(memory_space=pltpu.VMEM)
    smem = pl.BlockSpec(memory_space=pltpu.SMEM)
    dma = pltpu.SemaphoreType.DMA
    w_copies = 3 * (nx - 1 + ny - 1)
    input_grads, adam_step = pl.pallas_call(
        functools.partial(kernel, experts, nx, ny),
        out_shape=(
            jax.ShapeDtypeStruct((row_count, width), BF16),
            jax.ShapeDtypeStruct((mats, seg, hidden), F32),
        ),
        in_specs=[vmem, vmem, vmem, vmem, vmem, smem, smem, vmem],
        out_specs=(vmem, vmem),
        scratch_shapes=[
            pltpu.VMEM((slots, row_count), BF16),
            pltpu.VMEM((experts, cap, width), BF16),
            pltpu.VMEM((experts, cap, width), BF16),
            pltpu.VMEM((experts, cap, width), BF16),
            pltpu.VMEM((experts, cap, width), BF16),
            pltpu.VMEM((slots, width), BF16),
            pltpu.VMEM((mats, nx, ny, seg, hidden), BF16),
            pltpu.VMEM((slots, hidden), F32),
            pltpu.VMEM((slots, hidden), F32),
            pltpu.VMEM((slots, hidden), BF16),
            pltpu.VMEM((slots, hidden), BF16),
            pltpu.VMEM((slots, hidden), BF16),
            pltpu.VMEM((reps, mats * seg, hidden), BF16),
            pltpu.VMEM((reps, mats * seg, hidden), BF16),
            pltpu.VMEM((reps * reps, 8, 128), F32),
            pltpu.VMEM((reps, 128), F32),
            pltpu.VMEM((reps, reps, 128), F32),
            dma((experts,)), dma((experts,)), dma((experts,)), dma((experts,)),
            dma((w_copies,)), dma((w_copies,)),
            dma((reps,)), dma((reps,)), dma((reps,)), dma((reps,)),
        ],
        compiler_params=pltpu.CompilerParams(collective_id=0, has_side_effects=True),
        name="expert_step",
    )(
        weights[0], first_moment[0], second_moment[0], out_grads[0],
        routes.reshape(1, row_count), task_ids, task_weights, saved_inputs[0, 0],
    )
    return (input_grads[None], adam_step[None])


def solution(mesh):
    return jax.shard_map(
        shards,
        mesh=mesh,
        in_specs=(
            P("expert", None, "replica", None),
            P("expert", None, "replica", None),
            P("expert", None, "replica", None),
            P("replica", "expert", None),
            P("replica", "expert", None),
            P("replica", "expert"),
            P(),
            P("replica", "expert", None, None),
        ),
        out_specs=(P("replica", "expert", None), P("expert", None, "replica", None)),
        check_vma=False,
    )
```

```python
import functools

import jax
import jax.numpy as jnp
from jax import lax
from jax.experimental import pallas as pl
from jax.experimental.pallas import tpu as pltpu
from jax.sharding import PartitionSpec as P

beta_first = 0.9
beta_second = 0.95
adam_eps = 1e-08
norm_eps = 1e-06
first_fix = 1.0 - (0.9**50) ** 2
second_fix = 1.0 - (0.95**50) ** 2

F32 = jnp.float32
BF16 = jnp.bfloat16


def dot_rows(left, right):
    return lax.dot_general(left, right, (((0,), (0,)), ((), ())), preferred_element_type=F32)


def dot_last(left, right):
    return lax.dot_general(left, right, (((1,), (1,)), ((), ())), preferred_element_type=F32)


def iota(shape, axis):
    return lax.broadcasted_iota(jnp.int32, shape, axis)


def kernel(
    experts, nx, ny,
    w_ref, fm_ref, sm_ref, og_ref, route_ref, tid_ref, tw_ref, x_ref,
    ig_ref, step_ref,
    place, out3, in3, ret3, back3, rows, wfull, gact, upfac, gg, ug, hid, vsend, vbuf, acc, gsend, gbuf,
    a_send, a_recv, b_send, b_recv, w_send, w_recv, v_send, v_recv, g_send, g_recv,
):
    reps = nx * ny
    me_e = lax.axis_index("expert")
    me_r = lax.axis_index("replica")
    mx, my = me_r // ny, me_r % ny
    row_count, width = og_ref.shape
    slots = x_ref.shape[0]
    cap = slots // experts
    hidden = w_ref.shape[2]
    seg = w_ref.shape[1]
    half = seg // 2

    barrier = pltpu.get_barrier_semaphore()

    @pl.loop(1, experts)
    def _(i):
        pl.semaphore_signal(barrier, inc=1, device_id={"expert": (me_e + i) % experts, "replica": me_r})

    @pl.loop(1, reps)
    def _(i):
        pl.semaphore_signal(barrier, inc=1, device_id={"expert": me_e, "replica": (me_r + i) % reps})

    scale = tw_ref[tid_ref[0, 0]]
    expert_of = route_ref[...]
    chosen = (iota((experts, row_count), 0) == expert_of).astype(F32)
    earlier = (iota((row_count, row_count), 0) < iota((row_count, row_count), 1)).astype(BF16)
    before = jnp.dot(chosen.astype(BF16), earlier, preferred_element_type=F32)
    rank = jnp.sum(before * chosen, axis=0, keepdims=True)
    slot = expert_of * cap + rank.astype(jnp.int32)
    place[...] = (iota((slots, row_count), 0) == slot).astype(BF16)
    cols = min(512, width)
    for c in range(0, width, cols):
        scaled = (og_ref[:, c : c + cols].astype(F32) * scale).astype(BF16)
        moved = jnp.dot(place[...], scaled, preferred_element_type=F32)
        out3[:, :, c : c + cols] = moved.reshape(experts, cap, cols).astype(BF16)

    wfull[:, mx, my] = w_ref[...]
    pl.semaphore_wait(barrier, experts - 1 + reps - 1)

    def stage_one(k, along_y):
        lo = 0 if along_y else half
        idx = (0 if along_y else ny - 1) + k - 1
        to = mx * ny + (my + k) % ny if along_y else ((mx + k) % nx) * ny + my
        part = wfull.at[:, mx, my, lo : lo + half]
        return pltpu.make_async_remote_copy(
            src_ref=w_ref.at[:, lo : lo + half], dst_ref=part, send_sem=w_send.at[idx], recv_sem=w_recv.at[idx],
            device_id={"expert": me_e, "replica": to},
        )

    def stage_two(k, along_y, group):
        lo = half if along_y else 0
        base = (ny - 1) + (nx - 1)
        idx = base + (0 if along_y else ny - 1) + k - 1 + group * base
        to = mx * ny + (my + k) % ny if along_y else ((mx + k) % nx) * ny + my
        mats = pl.ds(0, 2) if group == 0 else pl.ds(2, 1)
        if along_y:
            part = wfull.at[mats, :, my, lo : lo + half]
        else:
            part = wfull.at[mats, mx, :, lo : lo + half]
        return pltpu.make_async_remote_copy(
            src_ref=part, dst_ref=part, send_sem=w_send.at[idx], recv_sem=w_recv.at[idx],
            device_id={"expert": me_e, "replica": to},
        )

    ones = [stage_one(k, True) for k in range(1, ny)] + [stage_one(k, False) for k in range(1, nx)]
    for c in ones:
        c.start()

    def row_copy(i, src, dst, send, recv):
        to = (me_e + i) % experts
        return pltpu.make_async_remote_copy(
            src_ref=src.at[to], dst_ref=dst.at[me_e], send_sem=send.at[i], recv_sem=recv.at[i],
            device_id={"expert": to, "replica": me_r},
        )

    def row_order(n):
        return (n + experts // 2) % experts

    @pl.loop(0, experts)
    def _(n):
        i = row_order(n)

        @pl.when(i != 0)
        def _():
            row_copy(i, out3, in3, a_send, a_recv).start()

    in3[me_e] = out3[me_e]

    for c in ones:
        c.wait_recv()
    twos = [
        [stage_two(k, True, g) for k in range(1, ny)] + [stage_two(k, False, g) for k in range(1, nx)]
        for g in range(2)
    ]
    for g in range(2):
        for c in twos[g]:
            c.start()

    for c in twos[0]:
        c.wait_recv()

    def weight(i):
        return wfull[i].reshape(reps * seg, hidden)

    xs = x_ref[...]
    gact[...] = jnp.dot(xs, weight(0), preferred_element_type=F32)
    upfac[...] = jnp.dot(xs, weight(1), preferred_element_type=F32)
    step_rows = 16

    @pl.loop(0, slots // step_rows)
    def _(n):
        at = pl.ds(pl.multiple_of(n * step_rows, step_rows), step_rows)
        gate, up = gact[at], upfac[at]
        sig = jax.nn.sigmoid(gate)
        act = gate * sig
        hid[at] = (act * up).astype(BF16)
        upfac[at] = up * sig * (1.0 + gate * (1.0 - sig))
        gact[at] = act

    for c in twos[1]:
        c.wait_recv()

    @pl.loop(1, experts)
    def _(i):
        row_copy(i, out3, in3, a_send, a_recv).wait_recv()

    def flat_rows(src):
        @pl.loop(0, slots // 16)
        def _(n):
            per = 16 // cap
            got = src[pl.ds(n * per, per)].astype(F32).reshape(16, width)
            rows[pl.ds(pl.multiple_of(n * 16, 16), 16)] = got.astype(BF16)

    order = sorted(
        [(dx, dy) for dx in range(nx) for dy in range(ny)],
        key=lambda o: (min(o[0], nx - o[0]) + min(o[1], ny - o[1]), o) if o != (0, 0) else (nx + ny, o),
    )
    code_x = sum(dx << (2 * k) for k, (dx, _) in enumerate(order))
    code_y = sum(dy << (2 * k) for k, (_, dy) in enumerate(order))
    own_k = reps - 1

    def offsets(k):
        return (jnp.int32(code_x) >> (2 * k)) & 3, (jnp.int32(code_y) >> (2 * k)) & 3

    def seg_copy(k, m):
        dx, dy = offsets(k)
        to = ((mx + dx) % nx) * ny + (my + dy) % ny
        sem = m * reps + k
        return pltpu.make_async_remote_copy(
            src_ref=vsend.at[m, to], dst_ref=vbuf.at[m, me_r], send_sem=v_send.at[sem], recv_sem=v_recv.at[sem],
            device_id={"expert": me_e, "replica": to},
        )

    def make_segments(m, left, right):
        @pl.loop(0, reps)
        def _(k):
            dx, dy = offsets(k)
            to = ((mx + dx) % nx) * ny + (my + dy) % ny
            at = pl.ds(pl.multiple_of(to * seg, seg), seg)
            vsend[m, to] = dot_rows(left[:, at], right[...]).astype(BF16)

            @pl.when(k != own_k)
            def _():
                seg_copy(k, m).start()

            @pl.when(k == own_k)
            def _():
                vbuf[m, me_r] = vsend[m, me_r]

    flat_rows(in3)
    make_segments(2, rows, hid)
    hidden_grad = jnp.dot(rows[...], weight(2), preferred_element_type=F32)
    gg[...] = (hidden_grad * upfac[...]).astype(BF16)
    ug[...] = (hidden_grad * gact[...]).astype(BF16)

    per = min(2, reps)

    @pl.loop(0, reps // per)
    def _(n):
        g_part = wfull[0, n * per // ny, pl.ds((n * per) % ny, per)].reshape(per * seg, hidden)
        u_part = wfull[1, n * per // ny, pl.ds((n * per) % ny, per)].reshape(per * seg, hidden)
        total = dot_last(gg[...], g_part) + dot_last(ug[...], u_part)
        at = pl.ds(pl.multiple_of(n * per * seg, per * seg), per * seg)
        ret3[:, :, at] = total.reshape(experts, cap, per * seg).astype(BF16)

    @pl.loop(1, experts)
    def _(i):
        row_copy(i, out3, in3, a_send, a_recv).wait_send()

    @pl.loop(0, experts)
    def _(n):
        i = row_order(n)

        @pl.when(i != 0)
        def _():
            row_copy(i, ret3, back3, b_send, b_recv).start()

    back3[me_e] = ret3[me_e]

    make_segments(0, x_ref, gg)
    make_segments(1, x_ref, ug)

    def from_replica(k):
        dx, dy = offsets(k)
        return ((mx + nx - dx) % nx) * ny + (my + ny - dy) % ny

    lanes = hidden // 128
    acc[...] = jnp.zeros_like(acc)

    @pl.loop(0, 3)
    def _(n):
        m = (n + 2) % 3

        @pl.loop(0, reps)
        def _(k):
            @pl.when(k != own_k)
            def _():
                seg_copy(k, m).wait_recv()

            r = from_replica(k)

            @pl.loop(0, k + 1)
            def _(j):
                s = from_replica(j)
                sums = [acc[r * reps + s]] + [jnp.zeros((8, 128), F32)] * (lanes - 1)
                for i in range(0, seg, 16):
                    product = vbuf[m, r, i : i + 16].astype(F32) * vbuf[m, s, i : i + 16].astype(F32)
                    for c in range(lanes):
                        column = product[:, c * 128 : (c + 1) * 128]
                        sums[c] = sums[c] + column[0:8] + column[8:16]
                total = sums[0]
                for c in range(1, lanes):
                    total = total + sums[c]
                acc[r * reps + s] = total
                acc[s * reps + r] = total

    lane = iota((reps, 128), 1)
    gram = jnp.zeros((reps, 128), F32)
    for r in range(reps):
        part = jnp.sum(acc[r * reps : (r + 1) * reps], axis=1)
        gram = gram + jnp.where(lane == r, jnp.sum(part, axis=1, keepdims=True), 0.0)
    gsend[...] = gram
    gbuf[me_r] = gram

    def gram_copy(i):
        to = (me_r + i) % reps
        return pltpu.make_async_remote_copy(
            src_ref=gsend, dst_ref=gbuf.at[me_r], send_sem=g_send.at[i], recv_sem=g_recv.at[i],
            device_id={"expert": me_e, "replica": to},
        )

    pl.loop(1, reps)(lambda i: gram_copy(i).start())

    @pl.loop(1, experts)
    def _(i):
        row_copy(i, ret3, back3, b_send, b_recv).wait_recv()

    flat_rows(back3)
    for c in range(0, width, cols):
        ig_ref[:, c : c + cols] = dot_rows(place[...], rows[:, c : c + cols]).astype(BF16)

    pl.loop(1, reps)(lambda i: gram_copy(i).wait_recv())
    total = gbuf[0]
    for r in range(1, reps):
        total = total + gbuf[r]
    gram = total[:, 0:reps]
    low, high = iota((reps, reps), 0), iota((reps, reps), 1)
    c_col = jnp.ones((reps, 1), F32)
    c_row = jnp.ones((1, reps), F32)
    for level in range(reps.bit_length() - 1):
        now = c_col * c_row * gram
        same = (low >> level) == (high >> level)
        pair = ((low >> (level + 1)) == (high >> (level + 1))) & jnp.logical_not(same)
        own = jnp.where(same, now, 0.0)
        other = jnp.where(pair, now, 0.0)
        own_row, own_col = jnp.sum(own, axis=0, keepdims=True), jnp.sum(own, axis=1, keepdims=True)
        ab_row, ab_col = jnp.sum(other, axis=0, keepdims=True), jnp.sum(other, axis=1, keepdims=True)
        norm_col = jnp.sum(jnp.where(same, own_row, 0.0), axis=1, keepdims=True)
        norm_row = jnp.sum(jnp.where(same, own_col, 0.0), axis=0, keepdims=True)
        cross_col = jnp.sum(jnp.where(same, ab_row, 0.0), axis=1, keepdims=True)
        cross_row = jnp.sum(jnp.where(same, ab_col, 0.0), axis=0, keepdims=True)
        c_col = c_col * (1.0 - cross_col / (2.0 * (norm_col + norm_eps)))
        c_row = c_row * (1.0 - cross_row / (2.0 * (norm_row + norm_eps)))

    coefs = [c_row[:, r : r + 1] for r in range(reps)]

    for m in range(3):

        @pl.loop(0, seg // 16)
        def _(n):
            at = pl.ds(pl.multiple_of(n * 16, 16), 16)
            merged = jnp.zeros((16, hidden), F32)
            for r in range(reps):
                merged = merged + coefs[r] * vbuf[m, r, at].astype(F32)
            first = beta_first * fm_ref[m, at] + (1.0 - beta_first) * merged
            second = beta_second * sm_ref[m, at] + (1.0 - beta_second) * merged * merged
            step_ref[m, at] = first / first_fix / (jnp.sqrt(second / second_fix) + adam_eps)

    for c in ones + twos[0] + twos[1]:
        c.wait_send()

    @pl.loop(1, experts)
    def _(i):
        row_copy(i, ret3, back3, b_send, b_recv).wait_send()

    @pl.loop(0, reps)
    def _(k):
        @pl.when(k != own_k)
        def _():
            for m in range(3):
                seg_copy(k, m).wait_send()

    pl.loop(1, reps)(lambda i: gram_copy(i).wait_send())


def grid_of(reps):
    ny = 1 << ((reps.bit_length() - 1) // 2)
    return reps // ny, ny


def shards(
    weights, first_moment, second_moment, out_grads, routes, task_ids, task_weights, saved_inputs
):
    experts = lax.axis_size("expert")
    reps = lax.axis_size("replica")
    nx, ny = grid_of(reps)
    row_count, width = out_grads.shape[1:]
    _, mats, seg, hidden = weights.shape
    slots = saved_inputs.shape[2]
    cap = slots // experts
    vmem = pl.BlockSpec(memory_space=pltpu.VMEM)
    smem = pl.BlockSpec(memory_space=pltpu.SMEM)
    dma = pltpu.SemaphoreType.DMA
    w_copies = 3 * (nx - 1 + ny - 1)
    input_grads, adam_step = pl.pallas_call(
        functools.partial(kernel, experts, nx, ny),
        out_shape=(
            jax.ShapeDtypeStruct((row_count, width), BF16),
            jax.ShapeDtypeStruct((mats, seg, hidden), F32),
        ),
        in_specs=[vmem, vmem, vmem, vmem, vmem, smem, smem, vmem],
        out_specs=(vmem, vmem),
        scratch_shapes=[
            pltpu.VMEM((slots, row_count), BF16),
            pltpu.VMEM((experts, cap, width), BF16),
            pltpu.VMEM((experts, cap, width), BF16),
            pltpu.VMEM((experts, cap, width), BF16),
            pltpu.VMEM((experts, cap, width), BF16),
            pltpu.VMEM((slots, width), BF16),
            pltpu.VMEM((mats, nx, ny, seg, hidden), BF16),
            pltpu.VMEM((slots, hidden), F32),
            pltpu.VMEM((slots, hidden), F32),
            pltpu.VMEM((slots, hidden), BF16),
            pltpu.VMEM((slots, hidden), BF16),
            pltpu.VMEM((slots, hidden), BF16),
            pltpu.VMEM((mats, reps, seg, hidden), BF16),
            pltpu.VMEM((mats, reps, seg, hidden), BF16),
            pltpu.VMEM((reps * reps, 8, 128), F32),
            pltpu.VMEM((reps, 128), F32),
            pltpu.VMEM((reps, reps, 128), F32),
            dma((experts,)), dma((experts,)), dma((experts,)), dma((experts,)),
            dma((w_copies,)), dma((w_copies,)),
            dma((mats * reps,)), dma((mats * reps,)), dma((reps,)), dma((reps,)),
        ],
        compiler_params=pltpu.CompilerParams(collective_id=0, has_side_effects=True),
        name="expert_step",
    )(
        weights[0], first_moment[0], second_moment[0], out_grads[0],
        routes.reshape(1, row_count), task_ids, task_weights, saved_inputs[0, 0],
    )
    return (input_grads[None], adam_step[None])


def solution(mesh):
    return jax.shard_map(
        shards,
        mesh=mesh,
        in_specs=(
            P("expert", None, "replica", None),
            P("expert", None, "replica", None),
            P("expert", None, "replica", None),
            P("replica", "expert", None),
            P("replica", "expert", None),
            P("replica", "expert"),
            P(),
            P("replica", "expert", None, None),
        ),
        out_specs=(P("replica", "expert", None), P("expert", None, "replica", None)),
        check_vma=False,
    )
```
